32 devices in a mesh: ckpt: 4 (over x, core), wide: 8 (over z, y).
Axes of the slice: x: 2, y: 2, z: 4, core: 2. Of those that a mesh axis runs over, the one named last changes fastest.
Arguments:
- codes: bfloat16 [4, 8, 8192, 1024], P('ckpt', 'wide'), may hold values from -4 to 4
- scales: float32 [4, 8, 8192, 8], P('ckpt', 'wide'), may hold values from 0.5 to 5
- example_ids: int32 [8, 8192], P('wide'), may hold values from 0 to 8191, each once within a row
- targets: bfloat16 [1024, 4096], P('wide'), may hold values from -0.09375 to 0.09375
- owners: int32 [6], replicated, may hold values from 0 to 7, as said below
Outputs:
- scores: float32 [8, 8192, 768], P('wide', 'ckpt')
The draws below stay inside these ranges and needn't reach their ends.
Inputs may be any that keep to these rules, and one draw needn't show every extreme that they name: `example_ids`: each row is a permutation of the 8192 examples of its group. Distinct owners; owner 0 and owner 8 - 1 are always among them.
All inputs are finite; a program needn't handle non-finite values.
Results may differ from the reference program's by a relative error of at most 0.0029.
Values may be sent and summed in bfloat16 or wider, within the bound.
A program may use at most 192 MiB of HBM per device.

```python
import math
import jax
import jax.numpy as jnp
from jax import lax

K = 1024
C = 4
QB = 128
TBLK = 128
ROUNDS = 6
GROUPS = 8
GROUP_ROWS = 8192
TARGETS = 768
OWNED = 1024
CK = 4096
QBLOCKS = 8


def draw_owners(key, part):
    first_key = jax.random.fold_in(key, 17)
    second_key = jax.random.fold_in(key, 29)
    middle = 1 + jax.random.permutation(first_key, GROUPS - 2).astype(jnp.int32)
    picked = jnp.concatenate([middle[:ROUNDS - 2], jnp.array([0, GROUPS - 1], jnp.int32)])
    return jax.random.permutation(second_key, picked).astype(jnp.int32)


def shard_levels(stream_key, extent, pieces, low, high):
    factor_of = 1.0
    for dim, shards_of in pieces:
        draws = jax.random.uniform(jax.random.fold_in(jax.random.fold_in(stream_key, 6), dim), (shards_of,), jnp.float32, low / len(pieces), high / len(pieces))
        factor_of = factor_of * jnp.repeat(jnp.exp(draws), extent[dim] // shards_of).reshape((-1,) + (1,) * (len(extent) - 1 - dim))
    return factor_of


def noise(key, extent, spread, most, cuts=(), kind=jnp.bfloat16):
    factor_of = shard_levels(key, extent, cuts, -0.22, 0.18) if cuts else 1.0
    entries = jax.random.normal(key, extent, jnp.float32) * spread * factor_of
    return jnp.minimum(jnp.maximum(entries, -most), most).astype(kind)


def setup_inputs(seed: int = 0) -> dict:
    splits = jax.random.split(jax.random.key(seed), 6)
    return {
        "codes": noise(splits[0], (C, GROUPS, GROUP_ROWS, K), 1.0, 4.0, ((0, 4), (1, 8))),
        "scales": jnp.clip(jnp.exp(math.log(5.0) - 2.3025851 * jax.random.uniform(splits[1], (C, GROUPS, GROUP_ROWS, QBLOCKS), jnp.float32) ** shard_levels(splits[1], (C, GROUPS, GROUP_ROWS, QBLOCKS), ((0, 4), (1, 8)), -0.2, 0.2)), 0.5, 5.0),
        "example_ids": jax.vmap(lambda own: jax.random.permutation(own, GROUP_ROWS))(jax.random.split(splits[2], GROUPS)).reshape((GROUPS, GROUP_ROWS)).astype(jnp.int32),
        "targets": noise(splits[3], (OWNED, CK), CK ** -0.5, 0.09375, ((0, 8),)),
        "owners": draw_owners(jax.random.fold_in(splits[5], 71), 0),
    }


def reference(codes, scales, example_ids, targets, owners):
    blocks = targets.reshape(GROUPS, TBLK, CK)
    chosen = jnp.take(blocks, owners, axis=0).reshape(TARGETS, CK)

    def one_group(group):
        group_codes = lax.dynamic_index_in_dim(codes, group, 1, keepdims=False)
        group_scales = lax.dynamic_index_in_dim(scales, group, 1, keepdims=False)
        feats = (group_codes.astype(jnp.float32) * jnp.repeat(group_scales, QB, axis=-1)).astype(jnp.bfloat16)
        ids = lax.dynamic_index_in_dim(example_ids, group, 0, keepdims=False)
        picked = jnp.take(feats, ids, axis=1)
        resident = jnp.transpose(picked, (1, 0, 2)).reshape(GROUP_ROWS, CK)
        total = lax.dot_general(resident, chosen, (((1,), (1,)), ((), ())), preferred_element_type=jnp.float32)
        return total * (1.0 / C)

    return lax.map(one_group, jnp.arange(GROUPS, dtype=jnp.int32))
```

```python
import functools

import jax
import jax.numpy as jnp
from jax import lax
from jax.experimental import pallas as pl
from jax.experimental.pallas import tpu as pltpu
from jax.sharding import PartitionSpec as P

TILE = 512
UNROLL = 32
SUBS = 2
DEPTH = 4
MESH = pl.DeviceIdType.MESH


def score_kernel(
    size,
    line,
    ids,
    owners,
    scales,
    codes,
    targets,
    out,
    feats,
    lhs,
    every,
    rhs,
    spread,
    picked,
    pair,
    summed,
    crossed,
    nearby,
    near,
    ready,
    tile_sem,
    own_sem,
    out_sem,
    up_send,
    down_send,
    over_send,
    line_recv,
    over_recv,
    pair_send,
    pair_recv,
    cross_send,
    cross_recv,
    near_recv,
):
    me = lax.axis_index("ckpt")
    w = lax.axis_index("wide")
    u, v = w // 2, w % 2
    core = me % 2
    mate = me + 1 - 2 * core
    chip = me // 2
    across = me + 2 - 4 * chip
    rows, width = codes.shape
    blocks = scales.shape[0]
    block = width // blocks
    own_rows = rows // size
    rounds = owners.shape[0]
    per_owner = targets.shape[0]
    extent = pair.shape[2]
    steps = own_rows // extent
    tiles = rows // TILE
    last = 2 * line - 1
    half = (2 * u) // line
    sub = per_owner // SUBS

    def tile_copy(t):
        slot = lax.rem(t, DEPTH)
        return pltpu.make_async_copy(
            codes.at[pl.ds(t * TILE, TILE), :],
            lhs.at[pl.ds(slot * TILE, TILE), :],
            tile_sem.at[slot],
        )

    own_copy = pltpu.make_async_copy(
        targets.at[:, pl.ds(pl.multiple_of(me * width, width), width)], every.at[w], own_sem
    )
    own_copy.start()
    for t in range(DEPTH - 1):
        tile_copy(t).start()

    flat = feats.reshape(rows * blocks, block)
    strided = picked.reshape(extent * blocks, block)

    barrier = pltpu.get_barrier_semaphore()
    for peer in ({"ckpt": mate}, {"ckpt": across}, {"wide": w + 1 - 2 * v}):
        pl.semaphore_signal(barrier, inc=1, device_id=peer, device_id_type=MESH)

    @pl.when(u + 1 < line)
    def greet_up():
        pl.semaphore_signal(barrier, inc=1, device_id={"wide": w + 2}, device_id_type=MESH)

    @pl.when(u >= 1)
    def greet_down():
        pl.semaphore_signal(barrier, inc=1, device_id={"wide": w - 2}, device_id_type=MESH)

    row_of = lax.broadcasted_iota(jnp.int32, spread.shape, 0) % blocks
    lane_of = lax.broadcasted_iota(jnp.int32, spread.shape, 1) // block
    spread[...] = jnp.where(row_of == lane_of, 1.0, 0.0).astype(spread.dtype)
    own_copy.wait()

    pl.semaphore_wait(barrier, 3 + jnp.minimum(u, 1) + jnp.minimum(line - 1 - u, 1))

    def piece(origin, s, send, recv, target):
        ref = every.at[origin * 2 + v, pl.ds(s * sub, sub), :]
        return pltpu.make_async_remote_copy(
            src_ref=ref,
            dst_ref=ref,
            send_sem=send.at[origin, s],
            recv_sem=recv.at[origin, s],
            device_id={"wide": target},
            device_id_type=MESH,
        )

    def up(origin, s):
        return piece(origin, s, up_send, line_recv, w + 2)

    def down(origin, s):
        return piece(origin, s, down_send, line_recv, w - 2)

    def over(origin, s):
        return piece(origin, s, over_send, over_recv, w + 1 - 2 * v)

    def came(origin, s):
        ref = every.at[origin * 2 + 1 - v, pl.ds(s * sub, sub), :]
        return pltpu.make_async_remote_copy(
            src_ref=ref,
            dst_ref=ref,
            send_sem=over_send.at[origin, s],
            recv_sem=over_recv.at[origin, s],
            device_id={"wide": w + 1 - 2 * v},
            device_id_type=MESH,
        )

    for s in range(SUBS):

        @pl.when(u + 1 < line)
        def send_up():
            up(u, s).start()

        @pl.when(u >= 1)
        def send_down():
            down(u, s).start()

        over(u, s).start()

    def relay(hop, s):
        @pl.when(u >= hop)
        def from_below():
            origin = u - hop
            up(origin, s).wait_recv()

            @pl.when(u + 1 < line)
            def on():
                up(origin, s).start()

            over(origin, s).start()

        @pl.when(u + hop < line)
        def from_above():
            origin = u + hop
            down(origin, s).wait_recv()

            @pl.when(u >= 1)
            def on():
                down(origin, s).start()

            over(origin, s).start()

    early = [(hop, s) for hop in range(1, min(3, line)) for s in range(SUBS)]
    polls = {(5 + 3 * k) * tiles // 16: e for k, e in enumerate(early)}
    middle = range(3, line // 2)
    late = range(max(3, line // 2), line)

    def scale(t, carry):
        @pl.when(t + DEPTH - 1 < tiles)
        def fetch():
            tile_copy(t + DEPTH - 1).start()

        tile_copy(t).wait()
        base = pl.multiple_of(lax.rem(t, DEPTH) * TILE, TILE)
        first = pl.multiple_of(t * TILE, TILE)
        whole = scales[:, pl.ds(first, TILE)]
        high = whole.astype(jnp.bfloat16).astype(jnp.float32)
        left = whole - high
        mid = left.astype(jnp.bfloat16).astype(jnp.float32)
        low = left - mid
        parts = jnp.concatenate([high, mid, low], 0).T.astype(jnp.bfloat16)
        factor = jnp.dot(parts, spread[...], preferred_element_type=jnp.float32)
        for q in range(blocks):
            span = slice(q * block, (q + 1) * block)
            value = lhs[pl.ds(base, TILE), span].astype(jnp.float32) * factor[:, span]
            value = value.astype(jnp.bfloat16).astype(jnp.float32)
            flat[pl.ds(first * blocks + q, TILE, stride=blocks), :] = value
        for at, (hop, s) in polls.items():

            @pl.when(t == at)
            def poll():
                relay(hop, s)

        return carry

    lax.fori_loop(0, tiles, scale, 0)
    for hop in middle:
        for s in range(SUBS):
            relay(hop, s)

    def gather(base, at):
        def some(i, carry):
            here = i * UNROLL
            got = [feats[ids[base + here + k]] for k in range(UNROLL)]
            for k in range(UNROLL):
                picked[here + k] = got[k]
            return carry

        lax.fori_loop(0, extent // UNROLL, some, 0)
        for q in range(blocks):
            lhs[pl.ds(at, extent), q * block : (q + 1) * block] = strided[
                pl.ds(q, extent, stride=blocks), :
            ].astype(jnp.bfloat16)

    def times(at, slot, count):
        return lax.dot_general(
            lhs[pl.ds(at, extent), :],
            rhs[slot * per_owner : (slot + count) * per_owner, :],
            (((1,), (1,)), ((), ())),
            preferred_element_type=jnp.float32,
        )

    def pair_copy(j, slot, count, into, recv):
        k = lax.rem(j, 2)
        return pltpu.make_async_remote_copy(
            src_ref=pair.at[k, pl.ds(0, count)],
            dst_ref=into.at[pl.ds(slot, count), pl.ds(j * extent, extent), :],
            send_sem=pair_send.at[k],
            recv_sem=recv,
            device_id={"ckpt": mate},
            device_id_type=MESH,
        )

    def cross_copy(phase, j, slot, count):
        span = pl.ds(j * extent, extent)
        return pltpu.make_async_remote_copy(
            src_ref=summed.at[pl.ds(slot, count), span, :],
            dst_ref=crossed.at[pl.ds(slot, count), span, :],
            send_sem=cross_send.at[phase, j],
            recv_sem=cross_recv.at[phase, j],
            device_id={"ckpt": across},
            device_id_type=MESH,
        )

    def far(phase, slot, count):
        diagonal = mate + 2 - 4 * chip

        def pair_part(j):
            at = pl.multiple_of(j * extent, extent)
            if phase == 0:
                gather(diagonal * own_rows + at, at)
            value = times(at, slot, count)

            @pl.when(j >= 2)
            def free():
                pair_copy(j, slot, count, summed, pair_recv.at[phase, j]).wait_send()

            k = lax.rem(j, 2)
            for c in range(count):
                pair[k, c] = value[:, c * per_owner : (c + 1) * per_owner].astype(pair.dtype)
            pair_copy(j, slot, count, summed, pair_recv.at[phase, j]).start()

        def own_part(j):
            at = pl.multiple_of(own_rows + j * extent, extent)
            here = pl.multiple_of(j * extent, extent)
            if phase == 0:
                gather(across * own_rows + here, at)
            value = times(at, slot, count)
            pair_copy(j, slot, count, summed, pair_recv.at[phase, j]).wait_recv()
            for c in range(count):
                part = value[:, c * per_owner : (c + 1) * per_owner]
                old = summed[slot + c, pl.ds(here, extent), :].astype(jnp.float32)
                summed[slot + c, pl.ds(here, extent), :] = (part + old).astype(summed.dtype)
            cross_copy(phase, j, slot, count).start()

        def step(j, carry):
            @pl.when(j < steps)
            def first():
                pair_part(j)

            @pl.when(j >= 1)
            def second():
                own_part(j - 1)

            if phase == 0:
                for s in range(SUBS):

                    @pl.when(j == 1 + 2 * s)
                    def poll():
                        for hop in late:
                            relay(hop, s)

            return carry

        lax.fori_loop(0, steps + 1, step, 0)
        for k in range(2):
            pair_copy(k, slot, count, summed, pair_recv.at[phase, k]).wait_send()

    crossing = (line - 1) * (1 - v)

    @pl.when(half != v)
    def near_edge():
        for s in range(SUBS):
            came(crossing, s).wait_recv()

    rhs[0:per_owner, :] = every[half * last]
    far(0, 0, 1)

    @pl.when(half == v)
    def far_edge():
        for s in range(SUBS):
            came(crossing, s).wait_recv()

    rhs[per_owner : 2 * per_owner, :] = every[(1 - half) * last]
    far(1, 1, 1)

    for origin in range(line):

        @pl.when(origin != crossing)
        def rest():
            for s in range(SUBS):
                came(origin, s).wait_recv()

    def unequal(a, b):
        return jnp.minimum((a - b) * (a - b), 1)

    slots = []
    chosen = [0] * rounds
    seen = jnp.int32(0)
    for r in range(rounds):
        owner = owners[r]
        edge = unequal(owner, half * last)
        inner = edge * unequal(owner, (1 - half) * last)
        slots.append(inner * (2 + seen) + (1 - inner) * edge)
        for k in range(rounds - 2):
            chosen[k] = chosen[k] + owner * inner * (1 - unequal(seen, k))
        seen = seen + inner
    for k in range(rounds - 2):
        rhs[(2 + k) * per_owner : (3 + k) * per_owner, :] = every[chosen[k]]
    far(2, 2, rounds - 2)

    def near_pair(j, carry):
        at = pl.multiple_of(lax.rem(j, 2) * extent, extent)
        gather(mate * own_rows + j * extent, at)
        value = times(at, 0, rounds)

        @pl.when(j >= 2)
        def free():
            pair_copy(j, 0, rounds, nearby, near_recv.at[j]).wait_send()

        k = lax.rem(j, 2)
        for c in range(rounds):
            pair[k, c] = value[:, c * per_owner : (c + 1) * per_owner].astype(pair.dtype)
        pair_copy(j, 0, rounds, nearby, near_recv.at[j]).start()
        return carry

    lax.fori_loop(0, steps, near_pair, 0)
    for k in range(2):
        pair_copy(k, 0, rounds, nearby, near_recv.at[k]).wait_send()

    def out_copy(j):
        k = lax.rem(j, 2)
        return pltpu.make_async_copy(
            ready.at[k], out.at[pl.ds(j * extent, extent), :], out_sem.at[k]
        )

    def near_own(j, carry):
        at = pl.multiple_of(lax.rem(j, 2) * extent, extent)
        gather(me * own_rows + j * extent, at)
        value = times(at, 0, rounds)
        pair_copy(j, 0, rounds, nearby, near_recv.at[j]).wait_recv()
        for c in range(rounds):
            part = value[:, c * per_owner : (c + 1) * per_owner]
            part = part + nearby[c, pl.ds(j * extent, extent), :].astype(jnp.float32)
            near[c] = part
        for phase, (slot, count) in enumerate(((0, 1), (1, 1), (2, rounds - 2))):
            cross_copy(phase, j, slot, count).wait_recv()

        for c in range(rounds):
            other = crossed[c, pl.ds(j * extent, extent), :].astype(jnp.float32)
            near[c] = (near[c] + other) * (1.0 / size)

        @pl.when(j >= 2)
        def free():
            out_copy(j - 2).wait()

        k = lax.rem(j, 2)
        for r in range(rounds):
            ready[k, :, r * per_owner : (r + 1) * per_owner] = near[slots[r]]
        out_copy(j).start()
        return carry

    lax.fori_loop(0, steps, near_own, 0)
    for j in range(max(0, steps - 2), steps):
        out_copy(j).wait()

    for phase, (slot, count) in enumerate(((0, 1), (1, 1), (2, rounds - 2))):

        def sent(j, carry):
            cross_copy(phase, j, slot, count).wait_send()
            return carry

        lax.fori_loop(0, steps, sent, 0)
    for origin in range(line):
        for s in range(SUBS):

            @pl.when((u >= origin) & (u + 1 < line))
            def sent_up():
                up(origin, s).wait_send()

            @pl.when((u <= origin) & (u >= 1))
            def sent_down():
                down(origin, s).wait_send()

            over(origin, s).wait_send()


def per_device(codes, scales, example_ids, targets, owners):
    size = lax.axis_size("ckpt")
    wide = lax.axis_size("wide")
    line = wide // 2
    rows, width = codes.shape[2:]
    blocks = scales.shape[3]
    block = width // blocks
    per_owner = targets.shape[0]
    rounds = owners.shape[0]
    own_rows = rows // size
    extent = own_rows // 8 if wide <= 8 else own_rows // 16
    steps = own_rows // extent
    dma = pltpu.SemaphoreType.DMA
    hbm = pl.BlockSpec(memory_space=pltpu.HBM)
    smem = pl.BlockSpec(memory_space=pltpu.SMEM)
    scores = pl.pallas_call(
        functools.partial(score_kernel, size, line),
        in_specs=[smem, smem, pl.BlockSpec(memory_space=pltpu.VMEM), hbm, hbm],
        out_specs=hbm,
        out_shape=jax.ShapeDtypeStruct((own_rows, rounds * per_owner), jnp.float32),
        scratch_shapes=[
            pltpu.VMEM((rows, blocks, block), jnp.float32),
            pltpu.VMEM((2 * own_rows, width), jnp.bfloat16),
            pltpu.VMEM((wide, per_owner, width), jnp.bfloat16),
            pltpu.VMEM((rounds * per_owner, width), jnp.bfloat16),
            pltpu.VMEM((3 * blocks, width), jnp.bfloat16),
            pltpu.VMEM((extent, blocks, block), jnp.float32),
            pltpu.VMEM((2, rounds, extent, per_owner), jnp.bfloat16),
            pltpu.VMEM((rounds, own_rows, per_owner), jnp.bfloat16),
            pltpu.VMEM((rounds, own_rows, per_owner), jnp.bfloat16),
            pltpu.VMEM((rounds, own_rows, per_owner), jnp.bfloat16),
            pltpu.VMEM((rounds, extent, per_owner), jnp.float32),
            pltpu.VMEM((2, extent, rounds * per_owner), jnp.float32),
            dma((DEPTH,)),
            dma,
            dma((2,)),
            dma((line, SUBS)),
            dma((line, SUBS)),
            dma((line, SUBS)),
            dma((line, SUBS)),
            dma((line, SUBS)),
            dma((2,)),
            dma((3, steps)),
            dma((3, steps)),
            dma((3, steps)),
            dma((steps,)),
        ],
        compiler_params=pltpu.CompilerParams(
            collective_id=0, has_side_effects=True, vmem_limit_bytes=67_043_328
        ),
    )(example_ids[0], owners, scales[0, 0].T, codes[0, 0], targets)
    return scores[None]


def solution(mesh):
    return jax.shard_map(
        per_device,
        mesh=mesh,
        in_specs=(
            P("ckpt", "wide", None, None),
            P("ckpt", "wide", None, None),
            P("wide", None),
            P("wide", None),
            P(),
        ),
        out_specs=P("wide", "ckpt", None),
        check_vma=False,
    )
```
